32 devices in a mesh: slab: 8 (over z, x), cross: 4 (over y, core).
Axes of the slice: x: 2, y: 2, z: 4, core: 2. Of those that a mesh axis runs over, the one named last changes fastest.
Arguments:
- les_state: float32 [54, 64, 16, 128], P(None, 'slab', 'cross'), may hold values from -6 to 6
- cmc_state: float32 [54, 128, 1024], P(None, 'cross', 'slab'), may hold values from -6 to 6
- cmc_map: int32 [64, 16, 128], P('slab', 'cross'), may hold values from 0 to 1023, as said below
- pdf_index: int32 [64, 16, 128], P('slab', 'cross'), may hold values from 0 to 127
- pdf_table: float32 [128, 128], replicated, may hold values from 0.001 to 0.05
- diffusion: float32 [54], replicated, may hold values from 0.02 to 0.15
- chem_matrix: float32 [54, 54], replicated, may hold values from -0.875 to 0.875
- dissipation: float32 [128, 1024], P('cross', 'slab'), may hold values from 0.05 to 0.2
- reaction_rate: float32 [128, 1024], P('cross', 'slab'), may hold values from 0.05 to 0.5
- substeps: int32 [1024], P('slab'), may hold values from 1 to 4
Outputs:
- les_out: float32 [54, 64, 16, 128], P(None, 'slab', 'cross')
- cmc_out: float32 [54, 128, 1024], P(None, 'cross', 'slab')
The draws below stay inside these ranges and needn't reach their ends.
Inputs may be any that keep to these rules, and one draw needn't show every extreme that they name: `cmc_map`: an LES cell in plane x along the jet axis maps to a CMC cell whose index divided by 128 differs from x divided by 8 (both rounded down) by at most one.
All inputs are finite; a program needn't handle non-finite values.
Results may differ from the reference program's by a relative error of at most 0.0001.
Values sent between devices are 32-bit elements; how exact they have to be, the bound alone decides.
A program may use at most 128 MiB of HBM per device.

```python
import math
import jax
import jax.numpy as jnp
from jax import lax

S = 54
NB = 128
NP = 128
CX = 8
CZ = 128
MC = 128
KMAX = 4
NX = 64
NY = 16
NCMC = 1024


def draw_cmc_map(key, part):
    plane = lax.broadcasted_iota(jnp.int32, (NX, NY, CZ), 0)
    base = plane // CX * MC + plane % CX * MC // CX
    jitter = jax.random.randint(key, (NX, NY, CZ), -MC, MC)
    return jnp.clip(base + jitter, 0, NCMC - 1).astype(jnp.int32)


def set_ends(values, own_key, low, top_value):
    shape = values.shape
    spot = [jax.random.randint(jax.random.fold_in(own_key, axis), (), 0, shape[axis]) for axis in range(len(shape))]
    values = values.at[tuple(spot)].set(low)
    longest = shape.index(max(shape))
    spot[longest] = (spot[longest] + 1) % shape[longest]
    return values.at[tuple(spot)].set(top_value)


def shard_levels(own_key, dims, cuts, least, largest):
    loudness, own = 1.0, jax.random.fold_in(own_key, 6)
    for position, shards_of in cuts:
        steps = jnp.exp(jax.random.uniform(jax.random.fold_in(own, position), (shards_of,), jnp.float32, least / len(cuts), largest / len(cuts)))
        loudness = loudness * jnp.repeat(steps, dims[position] // shards_of).reshape([-1 if axis == position else 1 for axis in range(len(dims))])
    return loudness


def gaussian(key, dims, scale, limit, split=(), held_as=jnp.bfloat16):
    array = jax.random.normal(key, dims, jnp.float32) * scale
    if len(split) > 0:
        array = shard_levels(key, dims, split, -0.22, 0.18) * array
    return jnp.clip(array, min=-limit, max=limit).astype(held_as)


def setup_inputs(seed: int = 0) -> dict:
    splits = jax.random.split(jax.random.key(seed), 11)
    les_state = gaussian(splits[0], (S, NX, NY, CZ), 1.0, 6.0, ((1, 8), (2, 4)), jnp.float32)
    cmc_state = gaussian(splits[1], (S, NB, NCMC), 1.0, 6.0, ((1, 4), (2, 8)), jnp.float32)
    cmc_map = draw_cmc_map(jax.random.fold_in(splits[10], 71), 0)
    pdf_index = set_ends(jax.random.randint(splits[3], (NX, NY, CZ), 0, NP), jax.random.fold_in(splits[3], 1), 0, NP - 1).astype(jnp.int32)
    pdf_table = jnp.clip(jnp.exp(jax.random.uniform(splits[4], (NP, NB), jnp.float32, math.log(0.001), math.log(0.05))), 0.001, 0.05)
    diffusion = jnp.clip(jnp.exp(jax.random.uniform(splits[5], (S,), jnp.float32, math.log(0.02), math.log(0.15))), 0.02, 0.15)
    chem_matrix = gaussian(splits[6], (S, S), S ** -0.5, 0.875, (), jnp.float32)
    dissipation = jnp.clip(0.05 + 0.15 * jax.random.uniform(splits[7], (NB, NCMC), jnp.float32) ** shard_levels(splits[7], (NB, NCMC), ((0, 4), (1, 8)), -0.2, 0.2), 0.05, 0.2)
    reaction_rate = jnp.clip(jnp.exp(math.log(0.5) - 2.3025851 * jax.random.uniform(splits[8], (NB, NCMC), jnp.float32) ** shard_levels(splits[8], (NB, NCMC), ((0, 4), (1, 8)), -0.2, 0.2)), 0.05, 0.5)
    substeps = set_ends(jax.random.randint(splits[9], (NCMC,), 1, KMAX + 1), jax.random.fold_in(splits[9], 1), 1, KMAX).astype(jnp.int32)
    return {"les_state": les_state, "cmc_state": cmc_state, "cmc_map": cmc_map, "pdf_index": pdf_index, "pdf_table": pdf_table, "diffusion": diffusion, "chem_matrix": chem_matrix, "dissipation": dissipation, "reaction_rate": reaction_rate, "substeps": substeps}


def reference(les_state, cmc_state, cmc_map, pdf_index, pdf_table, diffusion, chem_matrix, dissipation, reaction_rate, substeps):
    highest = lax.Precision.HIGHEST
    padded = jnp.pad(les_state, ((0, 0), (1, 1), (1, 1), (1, 1)))
    neighbours = padded[:, 2:, 1:-1, 1:-1] + padded[:, :-2, 1:-1, 1:-1]
    neighbours = neighbours + padded[:, 1:-1, 2:, 1:-1] + padded[:, 1:-1, :-2, 1:-1]
    neighbours = neighbours + padded[:, 1:-1, 1:-1, 2:] + padded[:, 1:-1, 1:-1, :-2]
    transported = les_state + diffusion[:, None, None, None] * (neighbours - 6.0 * les_state)
    species = transported.shape[0]
    flat = transported.reshape(species, -1)
    owner = cmc_map.reshape(-1).astype(jnp.int32)
    shape_id = pdf_index.reshape(-1).astype(jnp.int32)
    ncells = cmc_state.shape[2]
    nshape = pdf_table.shape[0]
    keys = owner * nshape + shape_id
    grouped = jax.ops.segment_sum(flat.T, keys, num_segments=ncells * nshape).reshape(ncells, nshape, species)
    counted = jax.ops.segment_sum(jnp.ones(owner.shape, jnp.float32), keys, num_segments=ncells * nshape).reshape(ncells, nshape)
    numer = jnp.einsum("mps,pb->sbm", grouped, pdf_table, precision=highest)
    denom = jnp.einsum("mp,pb->bm", counted, pdf_table, precision=highest)
    edged = jnp.pad(cmc_state, ((0, 0), (0, 0), (1, 1)))
    left_cells = edged[:, :, :-2]
    right_cells = edged[:, :, 2:]
    moved = cmc_state - 0.4 * (cmc_state - left_cells) + 0.1 * (right_cells - 2.0 * cmc_state + left_cells)
    blended = (numer + moved) / (denom[None] + 1.0)
    banded = jnp.pad(blended, ((0, 0), (1, 1), (0, 0)))
    state = blended + dissipation[None] * (banded[:, 2:] - 2.0 * blended + banded[:, :-2])
    for substep in range(KMAX):
        rate = jnp.dot(chem_matrix, state.reshape(species, -1), precision=highest).reshape(state.shape)
        active = (substep < substeps)[None, None, :]
        state = jnp.where(active, state + 0.5 * reaction_rate[None] * jnp.tanh(rate), state)
    projected = jnp.einsum("pb,sbm->spm", pdf_table, state, precision=highest).reshape(species, -1)
    conditional = jnp.take(projected, shape_id * ncells + owner, axis=1)
    weight_sum = jnp.sum(pdf_table, axis=1)
    conditional = conditional / weight_sum[shape_id][None, :]
    les_out = transported + 0.5 * (conditional.reshape(transported.shape) - transported)
    return les_out, state
```

```python
import functools

import jax
import jax.numpy as jnp
from jax import lax
from jax.experimental import pallas as pl
from jax.experimental.pallas import tpu as pltpu
from jax.sharding import PartitionSpec as P

KMAX = 4
F32 = jnp.float32
BF16 = jnp.bfloat16
NT = (((1,), (1,)), ((), ()))
NN = (((1,), (0,)), ((), ()))


def shift(array, axis, by):
    count = lax.axis_size(axis)
    return lax.ppermute(array, axis, [(i, i + by) for i in range(count) if 0 <= i + by < count])


def swap(array, axis, bit):
    count = lax.axis_size(axis)
    return lax.ppermute(array, axis, [(i, i ^ bit) for i in range(count)])


def halves(x):
    high = x.astype(BF16)
    return high, (x - high.astype(F32)).astype(BF16)


def decode(row, nshape):
    cell = jnp.floor((row + 0.5) * (1.0 / nshape))
    return cell.astype(jnp.int32), (row - cell * nshape).astype(jnp.int32)


def rows_equal(targets, row):
    return jnp.where(targets == row, 1.0, 0.0).astype(BF16)


def bin_kernel(bins, sp, cells, nshape, outer, first, *refs):
    if outer:
        t_ref, w_ref, *refs = refs
        acc_ref = None if first else refs.pop(0)
        out_ref, wc_ref, lhs = refs
    else:
        t_ref, wc_ref, *refs = refs
        acc_ref = None if first else refs.pop(0)
        out_ref, lhs = refs
    ct = t_ref.shape[1]

    @pl.when(pl.program_id(0) == 0)
    def _():
        out_ref[...] = jnp.zeros_like(out_ref) if first else acc_ref[...]

    t = t_ref[...]
    cell, shape = decode(t[sp - 1 : sp, :], nshape)
    if outer:
        ids = lax.broadcasted_iota(jnp.int32, (nshape, ct), 0)
        table = w_ref[...]
        high, low = halves(table)
        rest = (table - high.astype(F32) - low.astype(F32)).astype(BF16)
        split = jnp.concatenate([high.astype(F32), low.astype(F32), rest.astype(F32)], axis=0).astype(BF16)
        parts = lax.dot_general(split, rows_equal(ids, shape), NN, preferred_element_type=F32)
        wb = table.shape[0]
        wc = parts[:wb] + parts[wb : 2 * wb] + parts[2 * wb :]
        wc_ref[...] = wc
        targets = lax.broadcasted_iota(jnp.int32, (2 * cells, ct), 0)
        targets = jnp.where(targets >= cells, targets + cells, targets)
    else:
        wc = wc_ref[...]
        targets = lax.broadcasted_iota(jnp.int32, (cells, ct), 0) + cells
    for b in range(0, bins, 2):
        prod = jnp.concatenate([t * wc[b : b + 1, :], t * wc[b + 1 : b + 2, :]], axis=0)
        high, low = halves(prod)
        lhs[b * sp : (b + 2) * sp, :ct] = high
        lhs[b * sp : (b + 2) * sp, ct:] = low
    hot = rows_equal(targets, cell)
    hot = jnp.concatenate([hot, hot], axis=1)
    out_ref[...] += lax.dot_general(lhs[...], hot, NT, preferred_element_type=F32)


def bin_call(t, w, wc, acc, bins, cells, nshape, ct=512):
    sp, count = t.shape
    outer = wc is None
    width = (2 if outer else 1) * cells
    rows = bins * sp
    whole = lambda shape: pl.BlockSpec(shape, lambda i: (0,) * len(shape))
    col = lambda r: pl.BlockSpec((r, ct), lambda i: (0, i))
    wb = w.shape[0]
    args, specs = [t], [col(sp)]
    if outer:
        args.append(w)
        specs.append(whole(w.shape))
    else:
        args.append(wc)
        specs.append(col(wb))
    if acc is not None:
        args.append(acc)
        specs.append(whole(acc.shape))
    shapes = [jax.ShapeDtypeStruct((rows, width), F32)]
    outs = [whole((rows, width))]
    if outer:
        shapes.append(jax.ShapeDtypeStruct((wb, count), F32))
        outs.append(col(wb))
    flops = 4 * rows * width * count
    res = pl.pallas_call(
        functools.partial(bin_kernel, bins, sp, cells, nshape, outer, acc is None),
        grid=(count // ct,),
        out_shape=shapes,
        in_specs=specs,
        out_specs=outs,
        scratch_shapes=[pltpu.VMEM((rows, 2 * ct), BF16)],
        compiler_params=pltpu.CompilerParams(vmem_limit_bytes=40 << 20),
        cost_estimate=pl.CostEstimate(flops=flops, bytes_accessed=4 * sp * count, transcendentals=0),
        name="bin_outer" if outer else "bin_own",
    )(*args)
    return res if outer else res[0]


def chem_kernel(species, sp, own_ref, above_ref, below_ref, moved_ref, diss_ref, rate_ref, count_ref, matrix_ref, out_ref):
    bins = out_ref.shape[0]
    matrix = matrix_ref[...]
    count = count_ref[...]
    row = lax.broadcasted_iota(jnp.int32, (sp, out_ref.shape[2]), 0)

    def blend(b):
        total = own_ref[b] + above_ref[b] + below_ref[b]
        return (total + moved_ref[b]) / (total[species : species + 1, :] + 1.0)

    before, here = blend(0), blend(1)
    for b in range(bins):
        after = blend(b + 2)
        state = here + diss_ref[b : b + 1, :] * (after - 2.0 * here + before)
        half = 0.5 * rate_ref[b : b + 1, :]
        for k in range(KMAX):
            rate = lax.dot_general(matrix, state, NN, precision=lax.Precision.HIGHEST, preferred_element_type=F32)
            state = jnp.where(k < count, state + half * jnp.tanh(rate), state)
        out_ref[b] = jnp.where(row == species, 1.0, state)
        before, here = here, after


def project_kernel(bins, sp, cells, nshape, groups, accumulate, *refs):
    xs, refs = refs[: len(groups)], refs[len(groups) :]
    key_ref, wc_ref, *refs = refs
    acc_ref = refs.pop(0) if accumulate else None
    out_ref, lhs = refs
    ct = out_ref.shape[1]

    @pl.when(pl.program_id(0) == 0)
    def _():
        for n, x_ref in enumerate(xs):
            high, low = halves(x_ref[...])
            lhs[:, 2 * n * cells : (2 * n + 1) * cells] = high
            lhs[:, (2 * n + 1) * cells : (2 * n + 2) * cells] = low

    cell, _ = decode(key_ref[7:8, :], nshape)
    ids = lax.broadcasted_iota(jnp.int32, (cells, ct), 0)
    hots = []
    for g in groups:
        hot = rows_equal(ids + g * cells, cell)
        hots += [hot, hot]
    y = lax.dot_general(lhs[...], jnp.concatenate(hots, axis=0), NN, preferred_element_type=F32)
    total = acc_ref[...] if accumulate else jnp.zeros((sp, ct), F32)
    for b in range(bins):
        total = total + wc_ref[b + 1 : b + 2, :] * y[b * sp : (b + 1) * sp]
    out_ref[...] = total


def project_call(xs, groups, t, wc, acc, bins, cells, nshape, ct=256):
    sp, count = t.shape
    rows = bins * sp
    whole = lambda shape: pl.BlockSpec(shape, lambda i: (0,) * len(shape))
    col = lambda r: pl.BlockSpec((r, ct), lambda i: (0, i))
    args = list(xs) + [t, wc]
    specs = [whole(x.shape) for x in xs] + [pl.BlockSpec((8, ct), lambda i: (sp // 8 - 1, i)), col(wc.shape[0])]
    if acc is not None:
        args.append(acc)
        specs.append(col(sp))
    return pl.pallas_call(
        functools.partial(project_kernel, bins, sp, cells, nshape, groups, acc is not None),
        grid=(count // ct,),
        out_shape=jax.ShapeDtypeStruct((sp, count), F32),
        in_specs=specs,
        out_specs=col(sp),
        scratch_shapes=[pltpu.VMEM((rows, 2 * len(groups) * cells), BF16)],
        compiler_params=pltpu.CompilerParams(vmem_limit_bytes=40 << 20),
        cost_estimate=pl.CostEstimate(flops=4 * rows * cells * len(groups) * count, bytes_accessed=8 * sp * count, transcendentals=0),
        name="project",
    )(*args)


def on_device(
    les_state, cmc_state, cmc_map, pdf_index, pdf_table, diffusion, chem_matrix, dissipation, reaction_rate, substeps
):
    species = les_state.shape[0]
    sp = -(-(species + 2) // 8) * 8
    own_bins, cells = cmc_state.shape[1:]
    bins = own_bins + 2
    nshape = pdf_table.shape[0]
    count = cmc_map.size
    ncross = lax.axis_size("cross")

    below = shift(les_state[:, -1:], "slab", 1)
    above = shift(les_state[:, :1], "slab", -1)
    behind = shift(les_state[:, :, -1:], "cross", 1)
    ahead = shift(les_state[:, :, :1], "cross", -1)
    xs = jnp.concatenate([below, les_state, above], axis=1)
    ys = jnp.concatenate([behind, les_state, ahead], axis=2)
    zs = jnp.pad(les_state, ((0, 0), (0, 0), (0, 0), (1, 1)))
    around = xs[:, 2:] + xs[:, :-2] + ys[:, :, 2:] + ys[:, :, :-2] + zs[..., 2:] + zs[..., :-2]
    transported = les_state + diffusion[:, None, None, None] * (around - 6.0 * les_state)
    flat = transported.reshape(species, count)
    offset = cmc_map.reshape(1, count) - (lax.axis_index("slab") - 1) * cells
    key = (offset * nshape + pdf_index.reshape(1, count)).astype(F32)
    rows = [flat] + [jnp.ones((1, count), F32)] + [jnp.zeros((sp - species - 2, count), F32)] * (sp > species + 2) + [key]
    t_own = jnp.concatenate(rows, axis=0)

    wb = -(-bins // 8) * 8
    table = jnp.pad(pdf_table.T, ((1, wb - own_bins - 1), (0, 0)))
    table = lax.dynamic_slice_in_dim(table, lax.axis_index("cross") * own_bins, wb, axis=0)
    used = lax.broadcasted_iota(jnp.int32, (wb, 1), 0) < bins
    table = jnp.where(used, table, 0.0)

    blocks = [t_own]
    bits = [1 << k for k in range(ncross.bit_length() - 1)][::-1]
    for bit in bits:
        blocks.append(swap(jnp.concatenate(blocks, axis=1) if len(blocks) > 1 else blocks[0], "cross", bit))

    acc, wcs = None, []
    for block in blocks:
        acc, wc = bin_call(block, table, None, acc, bins, cells, nshape)
        wcs.append(wc)
    up = shift(acc[:, cells:], "slab", 1)
    down = shift(acc[:, :cells], "slab", -1)
    mine = None
    for block, wc in zip(blocks, wcs):
        mine = bin_call(block, table, wc, mine, bins, cells, nshape)

    left_cells = jnp.concatenate([shift(cmc_state[:, :, -1:], "slab", 1), cmc_state[:, :, :-1]], axis=2)
    right_cells = jnp.concatenate([cmc_state[:, :, 1:], shift(cmc_state[:, :, :1], "slab", -1)], axis=2)
    moved = cmc_state - 0.4 * (cmc_state - left_cells) + 0.1 * (right_cells - 2.0 * cmc_state + left_cells)
    moved = jnp.concatenate(
        [shift(moved[:, -1:], "cross", 1), moved, shift(moved[:, :1], "cross", -1)], axis=1
    )
    moved = jnp.pad(moved.transpose(1, 0, 2), ((0, 0), (0, sp - species), (0, 0)))

    cube = lambda a: a.reshape(bins, sp, cells)
    extra = sp - species
    fresh = pl.pallas_call(
        functools.partial(chem_kernel, species, sp),
        out_shape=jax.ShapeDtypeStruct((own_bins, sp, cells), F32),
        compiler_params=pltpu.CompilerParams(vmem_limit_bytes=40 << 20),
        name="chem",
    )(
        cube(mine), cube(up), cube(down), moved, dissipation, reaction_rate, substeps[None, :],
        jnp.pad(chem_matrix, ((0, extra), (0, extra))),
    )
    cmc_out = fresh[:, :species].transpose(1, 0, 2)
    fresh = fresh.reshape(own_bins * sp, cells)
    from_below = shift(fresh, "slab", 1)
    from_above = shift(fresh, "slab", -1)

    args = (own_bins, cells, nshape)
    own_part = [project_call([fresh], (1,), b, w, None, *args) for b, w in zip(blocks, wcs)]
    parts = [None] * len(blocks)
    for n in reversed(range(len(blocks))):
        parts[n] = project_call([from_below, from_above], (0, 2), blocks[n], wcs[n], own_part[n], *args)
    for n, bit in reversed(list(enumerate(bits))):
        got = swap(parts[n + 1], "cross", bit)
        parts[0 : n + 1] = [
            p + got[:, sum(q.shape[1] for q in parts[:k]) :][:, : p.shape[1]] for k, p in enumerate(parts[: n + 1])
        ]
    total = parts[0]
    conditional = (total[:species] / total[species : species + 1]).reshape(transported.shape)
    les_out = transported + 0.5 * (conditional - transported)
    return (les_out, cmc_out)


def solution(mesh):
    return jax.shard_map(
        on_device,
        mesh=mesh,
        in_specs=(
            P(None, "slab", "cross", None),
            P(None, "cross", "slab"),
            P("slab", "cross", None),
            P("slab", "cross", None),
            P(),
            P(),
            P(),
            P("cross", "slab"),
            P("cross", "slab"),
            P("slab"),
        ),
        out_specs=(P(None, "slab", "cross", None), P(None, "cross", "slab")),
        check_vma=False,
    )
```

```python
import functools

import jax
import jax.numpy as jnp
from jax import lax
from jax.experimental import pallas as pl
from jax.experimental.pallas import tpu as pltpu
from jax.sharding import PartitionSpec as P

KMAX = 4
F32 = jnp.float32
BF16 = jnp.bfloat16
NT = (((1,), (1,)), ((), ()))
NN = (((1,), (0,)), ((), ()))


def shift(array, axis, by):
    count = lax.axis_size(axis)
    return lax.ppermute(array, axis, [(i, i + by) for i in range(count) if 0 <= i + by < count])


def swap(array, axis, bit):
    count = lax.axis_size(axis)
    return lax.ppermute(array, axis, [(i, i ^ bit) for i in range(count)])


def halves(x):
    high = x.astype(BF16)
    return high, (x - high.astype(F32)).astype(BF16)


def decode(row, nshape):
    cell = jnp.floor((row + 0.5) * (1.0 / nshape))
    return cell.astype(jnp.int32), (row - cell * nshape).astype(jnp.int32)


def rows_equal(targets, row):
    return jnp.where(targets == row, 1.0, 0.0).astype(BF16)


def bin_kernel(bins, sp, cells, nshape, outer, first, *refs):
    if outer:
        t_ref, w_ref, *refs = refs
        acc_ref = None if first else refs.pop(0)
        out_ref, wc_ref, lhs = refs
    else:
        t_ref, wc_ref, *refs = refs
        acc_ref = None if first else refs.pop(0)
        out_ref, lhs = refs
    ct = t_ref.shape[1]

    @pl.when(pl.program_id(0) == 0)
    def _():
        out_ref[...] = jnp.zeros_like(out_ref) if first else acc_ref[...]

    t = t_ref[...]
    cell, shape = decode(t[sp - 1 : sp, :], nshape)
    if outer:
        ids = lax.broadcasted_iota(jnp.int32, (nshape, ct), 0)
        table = w_ref[...]
        high, low = halves(table)
        rest = (table - high.astype(F32) - low.astype(F32)).astype(BF16)
        split = jnp.concatenate([high.astype(F32), low.astype(F32), rest.astype(F32)], axis=0).astype(BF16)
        parts = lax.dot_general(split, rows_equal(ids, shape), NN, preferred_element_type=F32)
        wb = table.shape[0]
        wc = parts[:wb] + parts[wb : 2 * wb] + parts[2 * wb :]
        wc_ref[...] = wc
        targets = lax.broadcasted_iota(jnp.int32, (2 * cells, ct), 0)
        targets = jnp.where(targets >= cells, targets + cells, targets)
    else:
        wc = wc_ref[...]
        targets = lax.broadcasted_iota(jnp.int32, (cells, ct), 0) + cells
    for b in range(0, bins, 2):
        prod = jnp.concatenate([t * wc[b : b + 1, :], t * wc[b + 1 : b + 2, :]], axis=0)
        high, low = halves(prod)
        lhs[b * sp : (b + 2) * sp, :ct] = high
        lhs[b * sp : (b + 2) * sp, ct:] = low
    hot = rows_equal(targets, cell)
    hot = jnp.concatenate([hot, hot], axis=1)
    out_ref[...] += lax.dot_general(lhs[...], hot, NT, preferred_element_type=F32)


def bin_call(t, w, wc, acc, bins, cells, nshape, ct=512):
    sp, count = t.shape
    outer = wc is None
    width = (2 if outer else 1) * cells
    rows = bins * sp
    whole = lambda shape: pl.BlockSpec(shape, lambda i: (0,) * len(shape))
    col = lambda r: pl.BlockSpec((r, ct), lambda i: (0, i))
    wb = w.shape[0]
    args, specs = [t], [col(sp)]
    if outer:
        args.append(w)
        specs.append(whole(w.shape))
    else:
        args.append(wc)
        specs.append(col(wb))
    if acc is not None:
        args.append(acc)
        specs.append(whole(acc.shape))
    shapes = [jax.ShapeDtypeStruct((rows, width), F32)]
    outs = [whole((rows, width))]
    if outer:
        shapes.append(jax.ShapeDtypeStruct((wb, count), F32))
        outs.append(col(wb))
    flops = rows * width * count // 4
    res = pl.pallas_call(
        functools.partial(bin_kernel, bins, sp, cells, nshape, outer, acc is None),
        grid=(count // ct,),
        out_shape=shapes,
        in_specs=specs,
        out_specs=outs,
        scratch_shapes=[pltpu.VMEM((rows, 2 * ct), BF16)],
        compiler_params=pltpu.CompilerParams(vmem_limit_bytes=40 << 20),
        cost_estimate=pl.CostEstimate(flops=flops, bytes_accessed=4 * sp * count, transcendentals=0),
        name="bin_outer" if outer else "bin_own",
    )(*args)
    return res if outer else res[0]


def chem_kernel(species, sp, own_ref, above_ref, below_ref, moved_ref, diss_ref, rate_ref, count_ref, matrix_ref, out_ref):
    bins, _, cells = out_ref.shape
    third = matrix_ref.shape[1] // 3
    high, low = halves(matrix_ref[...])
    column = lax.broadcasted_iota(jnp.int32, matrix_ref.shape, 1)
    matrix = jnp.where(column < 2 * third, high.astype(F32), low.astype(F32)).astype(BF16)
    group = next(g for g in (4, 2, 1) if bins % g == 0)
    count = jnp.concatenate([count_ref[...]] * group, axis=1)
    row = lax.broadcasted_iota(jnp.int32, (sp, group * cells), 0)
    gap = [jnp.zeros((third - sp, group * cells), F32)] * (third > sp)

    def blend(b):
        total = own_ref[b] + above_ref[b] + below_ref[b]
        return (total + moved_ref[b]) / (total[species : species + 1, :] + 1.0)

    def wide(ref, b):
        return jnp.concatenate([ref[b + n : b + n + 1, :] for n in range(group)], axis=1)

    for b in range(0, bins, group):
        blends = [blend(b + n) for n in range(group + 2)]
        before, here, after = (jnp.concatenate(blends[n : n + group], axis=1) for n in range(3))
        state = here + wide(diss_ref, b) * (after - 2.0 * here + before)
        half = 0.5 * wide(rate_ref, b)
        for k in range(KMAX):
            high, low = (part.astype(F32) for part in halves(state))
            stack = jnp.concatenate([high, *gap, low, *gap, high, *gap], axis=0).astype(BF16)
            rate = lax.dot_general(matrix, stack, NN, preferred_element_type=F32)
            state = jnp.where(k < count, state + half * jnp.tanh(rate), state)
        state = jnp.where(row == species, 1.0, state)
        for n in range(group):
            out_ref[b + n] = state[:, n * cells : (n + 1) * cells]


def project_kernel(bins, sp, cells, nshape, groups, accumulate, *refs):
    xs, refs = refs[: len(groups)], refs[len(groups) :]
    key_ref, wc_ref, *refs = refs
    acc_ref = refs.pop(0) if accumulate else None
    out_ref, lhs = refs
    ct = out_ref.shape[1]

    @pl.when(pl.program_id(0) == 0)
    def _():
        for n, x_ref in enumerate(xs):
            high, low = halves(x_ref[...])
            lhs[:, 2 * n * cells : (2 * n + 1) * cells] = high
            lhs[:, (2 * n + 1) * cells : (2 * n + 2) * cells] = low

    cell, _ = decode(key_ref[7:8, :], nshape)
    ids = lax.broadcasted_iota(jnp.int32, (cells, ct), 0)
    hots = []
    for g in groups:
        hot = rows_equal(ids + g * cells, cell)
        hots += [hot, hot]
    y = lax.dot_general(lhs[...], jnp.concatenate(hots, axis=0), NN, preferred_element_type=F32)
    total = acc_ref[...] if accumulate else jnp.zeros((sp, ct), F32)
    for b in range(bins):
        total = total + wc_ref[b + 1 : b + 2, :] * y[b * sp : (b + 1) * sp]
    out_ref[...] = total


def project_call(xs, groups, t, wc, acc, bins, cells, nshape, ct=256):
    sp, count = t.shape
    rows = bins * sp
    whole = lambda shape: pl.BlockSpec(shape, lambda i: (0,) * len(shape))
    col = lambda r: pl.BlockSpec((r, ct), lambda i: (0, i))
    args = list(xs) + [t, wc]
    specs = [whole(x.shape) for x in xs] + [pl.BlockSpec((8, ct), lambda i: (sp // 8 - 1, i)), col(wc.shape[0])]
    if acc is not None:
        args.append(acc)
        specs.append(col(sp))
    return pl.pallas_call(
        functools.partial(project_kernel, bins, sp, cells, nshape, groups, acc is not None),
        grid=(count // ct,),
        out_shape=jax.ShapeDtypeStruct((sp, count), F32),
        in_specs=specs,
        out_specs=col(sp),
        scratch_shapes=[pltpu.VMEM((rows, 2 * len(groups) * cells), BF16)],
        compiler_params=pltpu.CompilerParams(vmem_limit_bytes=40 << 20),
        cost_estimate=pl.CostEstimate(flops=rows * cells * len(groups) * count // 4, bytes_accessed=8 * sp * count, transcendentals=0),
        name="project",
    )(*args)


def on_device(
    les_state, cmc_state, cmc_map, pdf_index, pdf_table, diffusion, chem_matrix, dissipation, reaction_rate, substeps
):
    species = les_state.shape[0]
    sp = -(-(species + 2) // 8) * 8
    own_bins, cells = cmc_state.shape[1:]
    bins = own_bins + 2
    nshape = pdf_table.shape[0]
    count = cmc_map.size
    ncross = lax.axis_size("cross")

    below = shift(les_state[:, -1:], "slab", 1)
    above = shift(les_state[:, :1], "slab", -1)
    behind = shift(les_state[:, :, -1:], "cross", 1)
    ahead = shift(les_state[:, :, :1], "cross", -1)
    xs = jnp.concatenate([below, les_state, above], axis=1)
    ys = jnp.concatenate([behind, les_state, ahead], axis=2)
    zs = jnp.pad(les_state, ((0, 0), (0, 0), (0, 0), (1, 1)))
    around = xs[:, 2:] + xs[:, :-2] + ys[:, :, 2:] + ys[:, :, :-2] + zs[..., 2:] + zs[..., :-2]
    transported = les_state + diffusion[:, None, None, None] * (around - 6.0 * les_state)
    flat = transported.reshape(species, count)
    offset = cmc_map.reshape(1, count) - (lax.axis_index("slab") - 1) * cells
    key = (offset * nshape + pdf_index.reshape(1, count)).astype(F32)
    rows = [flat] + [jnp.ones((1, count), F32)] + [jnp.zeros((sp - species - 2, count), F32)] * (sp > species + 2) + [key]
    t_own = jnp.concatenate(rows, axis=0)

    wb = -(-bins // 8) * 8
    table = jnp.pad(pdf_table.T, ((1, wb - own_bins - 1), (0, 0)))
    table = lax.dynamic_slice_in_dim(table, lax.axis_index("cross") * own_bins, wb, axis=0)
    used = lax.broadcasted_iota(jnp.int32, (wb, 1), 0) < bins
    table = jnp.where(used, table, 0.0)

    cmc_state, t_own = lax.optimization_barrier((cmc_state, t_own))
    left_cells = jnp.concatenate([shift(cmc_state[:, :, -1:], "slab", 1), cmc_state[:, :, :-1]], axis=2)
    right_cells = jnp.concatenate([cmc_state[:, :, 1:], shift(cmc_state[:, :, :1], "slab", -1)], axis=2)
    moved = cmc_state - 0.4 * (cmc_state - left_cells) + 0.1 * (right_cells - 2.0 * cmc_state + left_cells)
    moved = jnp.concatenate(
        [shift(moved[:, -1:], "cross", 1), moved, shift(moved[:, :1], "cross", -1)], axis=1
    )
    moved = jnp.pad(moved.transpose(1, 0, 2), ((0, 0), (0, sp - species), (0, 0)))

    blocks = [t_own]
    bits = [1 << k for k in range(ncross.bit_length() - 1)][::-1]
    for bit in bits:
        got = swap(jnp.concatenate(blocks, axis=1) if len(blocks) > 1 else blocks[0], "cross", bit)
        if len(blocks) == 1:
            got, moved = lax.optimization_barrier((got, moved))
        blocks.append(got)

    acc, wcs = None, []
    for block in blocks:
        acc, wc = bin_call(block, table, None, acc, bins, cells, nshape)
        wcs.append(wc)
    up = shift(acc[:, cells:], "slab", 1)
    down = shift(acc[:, :cells], "slab", -1)
    acc, *wcs = lax.optimization_barrier((acc, *wcs))
    mine = None
    for block, wc in zip(blocks, wcs):
        mine = bin_call(block, table, wc, mine, bins, cells, nshape)

    cube = lambda a: a.reshape(bins, sp, cells)
    extra = sp - species
    fresh = pl.pallas_call(
        functools.partial(chem_kernel, species, sp),
        out_shape=jax.ShapeDtypeStruct((own_bins, sp, cells), F32),
        compiler_params=pltpu.CompilerParams(vmem_limit_bytes=40 << 20),
        name="chem",
    )(
        cube(mine), cube(up), cube(down), moved, dissipation, reaction_rate, substeps[None, :],
        jnp.tile(jnp.pad(chem_matrix, ((0, extra), (0, -(-sp // 16) * 16 - species))), (1, 3)),
    )
    cmc_out = fresh[:, :species].transpose(1, 0, 2)
    fresh = fresh.reshape(own_bins * sp, cells)
    from_below = shift(fresh, "slab", 1)
    from_above = shift(fresh, "slab", -1)

    args = (own_bins, cells, nshape)
    own_part = [project_call([fresh], (1,), b, w, None, *args) for b, w in zip(blocks, wcs)]
    from_below, from_above, *own_part = lax.optimization_barrier((from_below, from_above, *own_part))
    parts = [None] * len(blocks)
    for n in reversed(range(len(blocks))):
        parts[n] = project_call([from_below, from_above], (0, 2), blocks[n], wcs[n], own_part[n], *args)
    for n, bit in reversed(list(enumerate(bits))):
        got = swap(parts[n + 1], "cross", bit)
        parts[0 : n + 1] = [
            p + got[:, sum(q.shape[1] for q in parts[:k]) :][:, : p.shape[1]] for k, p in enumerate(parts[: n + 1])
        ]
    total = parts[0]
    conditional = (total[:species] / total[species : species + 1]).reshape(transported.shape)
    les_out = transported + 0.5 * (conditional - transported)
    return (les_out, cmc_out)


def solution(mesh):
    return jax.shard_map(
        on_device,
        mesh=mesh,
        in_specs=(
            P(None, "slab", "cross", None),
            P(None, "cross", "slab"),
            P("slab", "cross", None),
            P("slab", "cross", None),
            P(),
            P(),
            P(),
            P("cross", "slab"),
            P("cross", "slab"),
            P("slab"),
        ),
        out_specs=(P(None, "slab", "cross", None), P(None, "cross", "slab")),
        check_vma=False,
    )
```

```python
import functools

import jax
import jax.numpy as jnp
from jax import lax
from jax.experimental import pallas as pl
from jax.experimental.pallas import tpu as pltpu
from jax.sharding import PartitionSpec as P

KMAX = 4
F32 = jnp.float32
BF16 = jnp.bfloat16
NT = (((1,), (1,)), ((), ()))
NN = (((1,), (0,)), ((), ()))


def shift(array, axis, by):
    count = lax.axis_size(axis)
    return lax.ppermute(array, axis, [(i, i + by) for i in range(count) if 0 <= i + by < count])


def swap(array, axis, bit):
    count = lax.axis_size(axis)
    return lax.ppermute(array, axis, [(i, i ^ bit) for i in range(count)])


def halves(x):
    high = x.astype(BF16)
    return high, (x - high.astype(F32)).astype(BF16)


def decode(row, nshape):
    cell = jnp.floor((row + 0.5) * (1.0 / nshape))
    return cell.astype(jnp.int32), (row - cell * nshape).astype(jnp.int32)


def rows_equal(targets, row):
    return jnp.where(targets == row, 1.0, 0.0).astype(BF16)


def bin_kernel(bins, sp, cells, nshape, outer, first, *refs):
    if outer:
        t_ref, w_ref, *refs = refs
        acc_ref = None if first else refs.pop(0)
        out_ref, wc_ref, lhs = refs
    else:
        t_ref, wc_ref, *refs = refs
        acc_ref = None if first else refs.pop(0)
        out_ref, lhs = refs
    ct = t_ref.shape[1]

    @pl.when(pl.program_id(0) == 0)
    def _():
        out_ref[...] = jnp.zeros_like(out_ref) if first else acc_ref[...]

    t = t_ref[...]
    cell, shape = decode(t[sp - 1 : sp, :], nshape)
    if outer:
        ids = lax.broadcasted_iota(jnp.int32, (nshape, ct), 0)
        table = w_ref[...]
        high, low = halves(table)
        rest = (table - high.astype(F32) - low.astype(F32)).astype(BF16)
        split = jnp.concatenate([high.astype(F32), low.astype(F32), rest.astype(F32)], axis=0).astype(BF16)
        parts = lax.dot_general(split, rows_equal(ids, shape), NN, preferred_element_type=F32)
        wb = table.shape[0]
        wc = parts[:wb] + parts[wb : 2 * wb] + parts[2 * wb :]
        wc_ref[...] = wc
        targets = lax.broadcasted_iota(jnp.int32, (2 * cells, ct), 0)
        targets = jnp.where(targets >= cells, targets + cells, targets)
    else:
        wc = wc_ref[...]
        targets = lax.broadcasted_iota(jnp.int32, (cells, ct), 0) + cells
    for b in range(0, bins, 2):
        prod = jnp.concatenate([t * wc[b : b + 1, :], t * wc[b + 1 : b + 2, :]], axis=0)
        high, low = halves(prod)
        lhs[b * sp : (b + 2) * sp, :ct] = high
        lhs[b * sp : (b + 2) * sp, ct:] = low
    hot = rows_equal(targets, cell)
    hot = jnp.concatenate([hot, hot], axis=1)
    out_ref[...] += lax.dot_general(lhs[...], hot, NT, preferred_element_type=F32)


def bin_call(t, w, wc, acc, bins, cells, nshape, ct=512):
    sp, count = t.shape
    outer = wc is None
    width = (2 if outer else 1) * cells
    rows = bins * sp
    whole = lambda shape: pl.BlockSpec(shape, lambda i: (0,) * len(shape))
    col = lambda r: pl.BlockSpec((r, ct), lambda i: (0, i))
    wb = w.shape[0]
    args, specs = [t], [col(sp)]
    if outer:
        args.append(w)
        specs.append(whole(w.shape))
    else:
        args.append(wc)
        specs.append(col(wb))
    if acc is not None:
        args.append(acc)
        specs.append(whole(acc.shape))
    shapes = [jax.ShapeDtypeStruct((rows, width), F32)]
    outs = [whole((rows, width))]
    if outer:
        shapes.append(jax.ShapeDtypeStruct((wb, count), F32))
        outs.append(col(wb))
    flops = rows * width * count // 4
    res = pl.pallas_call(
        functools.partial(bin_kernel, bins, sp, cells, nshape, outer, acc is None),
        grid=(count // ct,),
        out_shape=shapes,
        in_specs=specs,
        out_specs=outs,
        scratch_shapes=[pltpu.VMEM((rows, 2 * ct), BF16)],
        compiler_params=pltpu.CompilerParams(vmem_limit_bytes=40 << 20),
        cost_estimate=pl.CostEstimate(flops=flops, bytes_accessed=4 * sp * count, transcendentals=0),
        name="bin_outer" if outer else "bin_own",
    )(*args)
    return res if outer else res[0]


def chem_kernel(species, sp, own_ref, above_ref, below_ref, moved_ref, diss_ref, rate_ref, count_ref, matrix_ref, out_ref):
    bins, _, cells = out_ref.shape
    third = matrix_ref.shape[1] // 3
    high, low = halves(matrix_ref[...])
    column = lax.broadcasted_iota(jnp.int32, matrix_ref.shape, 1)
    matrix = jnp.where(column < 2 * third, high.astype(F32), low.astype(F32)).astype(BF16)
    group = next(g for g in (4, 2, 1) if bins % g == 0)
    count = jnp.concatenate([count_ref[...]] * group, axis=1)
    row = lax.broadcasted_iota(jnp.int32, (sp, group * cells), 0)
    gap = [jnp.zeros((third - sp, group * cells), F32)] * (third > sp)

    def blend(b):
        total = own_ref[b] + above_ref[b] + below_ref[b]
        return (total + moved_ref[b]) / (total[species : species + 1, :] + 1.0)

    def wide(ref, b):
        return jnp.concatenate([ref[b + n : b + n + 1, :] for n in range(group)], axis=1)

    for b in range(0, bins, group):
        blends = [blend(b + n) for n in range(group + 2)]
        before, here, after = (jnp.concatenate(blends[n : n + group], axis=1) for n in range(3))
        state = here + wide(diss_ref, b) * (after - 2.0 * here + before)
        half = 0.5 * wide(rate_ref, b)
        for k in range(KMAX):
            high, low = (part.astype(F32) for part in halves(state))
            stack = jnp.concatenate([high, *gap, low, *gap, high, *gap], axis=0).astype(BF16)
            rate = lax.dot_general(matrix, stack, NN, preferred_element_type=F32)
            state = jnp.where(k < count, state + half * jnp.tanh(rate), state)
        state = jnp.where(row == species, 1.0, state)
        for n in range(group):
            out_ref[b + n] = state[:, n * cells : (n + 1) * cells]


def project_kernel(bins, sp, cells, nshape, groups, accumulate, *refs):
    xs, refs = refs[: len(groups)], refs[len(groups) :]
    key_ref, wc_ref, *refs = refs
    acc_ref = refs.pop(0) if accumulate else None
    out_ref, lhs = refs
    ct = out_ref.shape[1]

    @pl.when(pl.program_id(0) == 0)
    def _():
        for n, x_ref in enumerate(xs):
            high, low = halves(x_ref[...])
            lhs[:, 2 * n * cells : (2 * n + 1) * cells] = high
            lhs[:, (2 * n + 1) * cells : (2 * n + 2) * cells] = low

    cell, _ = decode(key_ref[7:8, :], nshape)
    ids = lax.broadcasted_iota(jnp.int32, (cells, ct), 0)
    hots = []
    for g in groups:
        hot = rows_equal(ids + g * cells, cell)
        hots += [hot, hot]
    y = lax.dot_general(lhs[...], jnp.concatenate(hots, axis=0), NN, preferred_element_type=F32)
    total = acc_ref[...] if accumulate else jnp.zeros((sp, ct), F32)
    for b in range(bins):
        total = total + wc_ref[b + 1 : b + 2, :] * y[b * sp : (b + 1) * sp]
    out_ref[...] = total


def project_call(xs, groups, t, wc, acc, place, count, bins, cells, nshape, ct=256):
    sp, skip = t.shape[0], place // ct
    rows = bins * sp
    whole = lambda shape: pl.BlockSpec(shape, lambda i: (0,) * len(shape))
    col = lambda r: pl.BlockSpec((r, ct), lambda i: (0, i))
    args = list(xs) + [t, wc]
    specs = [whole(x.shape) for x in xs]
    specs.append(pl.BlockSpec((8, ct), lambda i: (sp // 8 - 1, i + skip)))
    specs.append(pl.BlockSpec((wc.shape[0], ct), lambda i: (0, i + skip)))
    if acc is not None:
        args.append(acc)
        specs.append(col(sp))
    return pl.pallas_call(
        functools.partial(project_kernel, bins, sp, cells, nshape, groups, acc is not None),
        grid=(count // ct,),
        out_shape=jax.ShapeDtypeStruct((sp, count), F32),
        in_specs=specs,
        out_specs=col(sp),
        scratch_shapes=[pltpu.VMEM((rows, 2 * len(groups) * cells), BF16)],
        compiler_params=pltpu.CompilerParams(vmem_limit_bytes=40 << 20),
        cost_estimate=pl.CostEstimate(flops=rows * cells * len(groups) * count // 4, bytes_accessed=8 * sp * count, transcendentals=0),
        name="project",
    )(*args)


def on_device(
    les_state, cmc_state, cmc_map, pdf_index, pdf_table, diffusion, chem_matrix, dissipation, reaction_rate, substeps
):
    species = les_state.shape[0]
    sp = -(-(species + 2) // 8) * 8
    own_bins, cells = cmc_state.shape[1:]
    bins = own_bins + 2
    nshape = pdf_table.shape[0]
    count = cmc_map.size
    ncross = lax.axis_size("cross")

    planes, ends = les_state.shape[1], les_state.shape[2] * les_state.shape[3]

    def slab_end(at):
        return jnp.concatenate([les_state[:, at].reshape(species, ends), cmc_state[:, :, at]], axis=1)

    from_left, from_right = shift(slab_end(-1), "slab", 1), shift(slab_end(0), "slab", -1)
    below, above = (g[:, :ends].reshape(les_state[:, :1].shape) for g in (from_left, from_right))
    left_end, right_end = from_left[:, ends:, None], from_right[:, ends:, None]

    def advect(state, left, right):
        left = jnp.concatenate([left, state[:, :, :-1]], axis=2)
        right = jnp.concatenate([state[:, :, 1:], right], axis=2)
        return state - 0.4 * (state - left) + 0.1 * (right - 2.0 * state + left)

    def cross_end(at):
        rows = les_state[:, :, at].reshape(species, -1)
        pick = slice(at, at + 1 or None)
        bin_row = advect(cmc_state[:, pick], left_end[:, pick], right_end[:, pick])
        return jnp.concatenate([rows, bin_row[:, 0]], axis=1)

    from_behind, from_ahead = shift(cross_end(-1), "cross", 1), shift(cross_end(0), "cross", -1)
    behind, ahead = (g[:, :-cells].reshape(les_state[:, :, :1].shape) for g in (from_behind, from_ahead))
    bin_before, bin_after = from_behind[:, None, -cells:], from_ahead[:, None, -cells:]
    xs = jnp.concatenate([below, les_state, above], axis=1)
    ys = jnp.concatenate([behind, les_state, ahead], axis=2)
    zs = jnp.pad(les_state, ((0, 0), (0, 0), (0, 0), (1, 1)))
    around = xs[:, 2:] + xs[:, :-2] + ys[:, :, 2:] + ys[:, :, :-2] + zs[..., 2:] + zs[..., :-2]
    transported = les_state + diffusion[:, None, None, None] * (around - 6.0 * les_state)
    flat = transported.reshape(species, count)
    offset = cmc_map.reshape(1, count) - (lax.axis_index("slab") - 1) * cells
    key = (offset * nshape + pdf_index.reshape(1, count)).astype(F32)
    rows = [flat] + [jnp.ones((1, count), F32)] + [jnp.zeros((sp - species - 2, count), F32)] * (sp > species + 2) + [key]
    t_own = jnp.concatenate(rows, axis=0)

    wb = -(-bins // 8) * 8
    table = jnp.pad(pdf_table.T, ((1, wb - own_bins - 1), (0, 0)))
    table = lax.dynamic_slice_in_dim(table, lax.axis_index("cross") * own_bins, wb, axis=0)
    used = lax.broadcasted_iota(jnp.int32, (wb, 1), 0) < bins
    table = jnp.where(used, table, 0.0)

    cmc_state, t_own = lax.optimization_barrier((cmc_state, t_own))
    moved = jnp.concatenate([bin_before, advect(cmc_state, left_end, right_end), bin_after], axis=1)
    moved = jnp.pad(moved.transpose(1, 0, 2), ((0, 0), (0, sp - species), (0, 0)))

    blocks, wcs = [t_own], []
    bits = [1 << k for k in range(ncross.bit_length() - 1)][::-1]
    acc, wc = bin_call(t_own, table, None, None, bins, cells, nshape)
    wcs.append(wc)
    for bit in bits:
        got = swap(jnp.concatenate(blocks, axis=1) if len(blocks) > 1 else blocks[0], "cross", bit)
        if len(blocks) == 1:
            got, moved, acc, wcs[0] = lax.optimization_barrier((got, moved, acc, wcs[0]))
        blocks.append(got)
    for block in blocks[1:]:
        acc, wc = bin_call(block, table, None, acc, bins, cells, nshape)
        wcs.append(wc)
    up = shift(acc[:, cells:], "slab", 1)
    down = shift(acc[:, :cells], "slab", -1)
    acc, *wcs = lax.optimization_barrier((acc, *wcs))
    mine = None
    for block, wc in zip(blocks, wcs):
        mine = bin_call(block, table, wc, mine, bins, cells, nshape)

    cube = lambda a: a.reshape(bins, sp, cells)
    extra = sp - species
    fresh = pl.pallas_call(
        functools.partial(chem_kernel, species, sp),
        out_shape=jax.ShapeDtypeStruct((own_bins, sp, cells), F32),
        compiler_params=pltpu.CompilerParams(vmem_limit_bytes=40 << 20),
        name="chem",
    )(
        cube(mine), cube(up), cube(down), moved, dissipation, reaction_rate, substeps[None, :],
        jnp.tile(jnp.pad(chem_matrix, ((0, extra), (0, -(-sp // 16) * 16 - species))), (1, 3)),
    )
    cmc_out = fresh[:, :species].transpose(1, 0, 2)
    fresh = fresh.reshape(own_bins * sp, cells)
    from_below = shift(fresh, "slab", 1)
    from_above = shift(fresh, "slab", -1)

    args = (count, own_bins, cells, nshape)
    where = [(blocks[0], wcs[0], 0)]
    for bit, block, wc in zip(bits, blocks[1:], wcs[1:]):
        held = {r: n for n, r in enumerate(order)} if bit != bits[0] else {0: 0}
        order = list(held) + [r ^ bit for r in held]
        where += [(block, wc, n * count) for n in range(len(held))]
    order = order if bits else [0]
    places = dict(zip(order, where))
    own_part = {r: project_call([fresh], (1,), *places[r][:2], None, places[r][2], *args) for r in order}
    from_below, from_above, own_part = lax.optimization_barrier((from_below, from_above, own_part))

    def reduced(who, bits, sides):
        if not bits:
            block, wc, place = places[who]
            return project_call(sides, (0, 2), block, wc, own_part[who], place, *args)
        far = reduced(who ^ bits[0], bits[1:], sides)
        if len(bits) > 1:
            far, sides = lax.optimization_barrier((far, sides))
        got = swap(far, "cross", bits[0])
        return reduced(who, bits[1:], sides) + got

    total = reduced(0, bits, [from_below, from_above])
    conditional = (total[:species] / total[species : species + 1]).reshape(transported.shape)
    les_out = transported + 0.5 * (conditional - transported)
    return (les_out, cmc_out)


def solution(mesh):
    return jax.shard_map(
        on_device,
        mesh=mesh,
        in_specs=(
            P(None, "slab", "cross", None),
            P(None, "cross", "slab"),
            P("slab", "cross", None),
            P("slab", "cross", None),
            P(),
            P(),
            P(),
            P("cross", "slab"),
            P("cross", "slab"),
            P("slab"),
        ),
        out_specs=(P(None, "slab", "cross", None), P(None, "cross", "slab")),
        check_vma=False,
    )
```

```python
import functools

import jax
import jax.numpy as jnp
from jax import lax
from jax.experimental import pallas as pl
from jax.experimental.pallas import tpu as pltpu
from jax.sharding import PartitionSpec as P

KMAX = 4
F32 = jnp.float32
BF16 = jnp.bfloat16
NT = (((1,), (1,)), ((), ()))
NN = (((1,), (0,)), ((), ()))


def shift(array, axis, by):
    count = lax.axis_size(axis)
    return lax.ppermute(array, axis, [(i, i + by) for i in range(count) if 0 <= i + by < count])


def swap(array, axis, bit):
    count = lax.axis_size(axis)
    return lax.ppermute(array, axis, [(i, i ^ bit) for i in range(count)])


def halves(x):
    high = x.astype(BF16)
    return high, (x - high.astype(F32)).astype(BF16)


def decode(row, nshape):
    cell = jnp.floor((row + 0.5) * (1.0 / nshape))
    return cell.astype(jnp.int32), (row - cell * nshape).astype(jnp.int32)


def rows_equal(targets, row):
    return jnp.where(targets == row, 1.0, 0.0).astype(BF16)


def bin_kernel(bins, sp, cells, nshape, outer, first, *refs):
    if outer:
        t_ref, w_ref, *refs = refs
        acc_ref = None if first else refs.pop(0)
        out_ref, wc_ref, lhs = refs
    else:
        t_ref, wc_ref, *refs = refs
        acc_ref = None if first else refs.pop(0)
        out_ref, lhs = refs
    ct = t_ref.shape[1]

    @pl.when(pl.program_id(0) == 0)
    def _():
        out_ref[...] = jnp.zeros_like(out_ref) if first else acc_ref[...]

    t = t_ref[...]
    cell, shape = decode(t[sp - 1 : sp, :], nshape)
    if outer:
        ids = lax.broadcasted_iota(jnp.int32, (nshape, ct), 0)
        table = w_ref[...]
        high, low = halves(table)
        rest = (table - high.astype(F32) - low.astype(F32)).astype(BF16)
        split = jnp.concatenate([high.astype(F32), low.astype(F32), rest.astype(F32)], axis=0).astype(BF16)
        parts = lax.dot_general(split, rows_equal(ids, shape), NN, preferred_element_type=F32)
        wb = table.shape[0]
        wc = parts[:wb] + parts[wb : 2 * wb] + parts[2 * wb :]
        wc_ref[...] = wc
        targets = lax.broadcasted_iota(jnp.int32, (2 * cells, ct), 0)
        targets = jnp.where(targets >= cells, targets + cells, targets)
    else:
        wc = wc_ref[...]
        targets = lax.broadcasted_iota(jnp.int32, (cells, ct), 0) + cells
    for b in range(0, bins, 2):
        prod = jnp.concatenate([t * wc[b : b + 1, :], t * wc[b + 1 : b + 2, :]], axis=0)
        high, low = halves(prod)
        lhs[b * sp : (b + 2) * sp, :ct] = high
        lhs[b * sp : (b + 2) * sp, ct:] = low
    hot = rows_equal(targets, cell)
    hot = jnp.concatenate([hot, hot], axis=1)
    out_ref[...] += lax.dot_general(lhs[...], hot, NT, preferred_element_type=F32)


def bin_call(t, w, wc, acc, bins, cells, nshape, ct=512):
    sp, count = t.shape
    outer = wc is None
    width = (2 if outer else 1) * cells
    rows = bins * sp
    whole = lambda shape: pl.BlockSpec(shape, lambda i: (0,) * len(shape))
    col = lambda r: pl.BlockSpec((r, ct), lambda i: (0, i))
    wb = w.shape[0]
    args, specs = [t], [col(sp)]
    if outer:
        args.append(w)
        specs.append(whole(w.shape))
    else:
        args.append(wc)
        specs.append(col(wb))
    if acc is not None:
        args.append(acc)
        specs.append(whole(acc.shape))
    shapes = [jax.ShapeDtypeStruct((rows, width), F32)]
    outs = [whole((rows, width))]
    if outer:
        shapes.append(jax.ShapeDtypeStruct((wb, count), F32))
        outs.append(col(wb))
    flops = rows * width * count // 4
    res = pl.pallas_call(
        functools.partial(bin_kernel, bins, sp, cells, nshape, outer, acc is None),
        grid=(count // ct,),
        out_shape=shapes,
        in_specs=specs,
        out_specs=outs,
        scratch_shapes=[pltpu.VMEM((rows, 2 * ct), BF16)],
        compiler_params=pltpu.CompilerParams(vmem_limit_bytes=40 << 20),
        cost_estimate=pl.CostEstimate(flops=flops, bytes_accessed=4 * sp * count, transcendentals=0),
        name="bin_outer" if outer else "bin_own",
    )(*args)
    return res if outer else res[0]


def chem_kernel(species, sp, own_ref, above_ref, below_ref, moved_ref, diss_ref, rate_ref, count_ref, matrix_ref, out_ref):
    bins, _, cells = out_ref.shape
    third = matrix_ref.shape[1] // 3
    high, low = halves(matrix_ref[...])
    column = lax.broadcasted_iota(jnp.int32, matrix_ref.shape, 1)
    matrix = jnp.where(column < 2 * third, high.astype(F32), low.astype(F32)).astype(BF16)
    group = next(g for g in (4, 2, 1) if bins % g == 0)
    count = jnp.concatenate([count_ref[...]] * group, axis=1)
    row = lax.broadcasted_iota(jnp.int32, (sp, group * cells), 0)
    gap = [jnp.zeros((third - sp, group * cells), F32)] * (third > sp)

    def blend(b):
        total = own_ref[b] + above_ref[b] + below_ref[b]
        return (total + moved_ref[b]) / (total[species : species + 1, :] + 1.0)

    def wide(ref, b):
        return jnp.concatenate([ref[b + n : b + n + 1, :] for n in range(group)], axis=1)

    for b in range(0, bins, group):
        blends = [blend(b + n) for n in range(group + 2)]
        before, here, after = (jnp.concatenate(blends[n : n + group], axis=1) for n in range(3))
        state = here + wide(diss_ref, b) * (after - 2.0 * here + before)
        half = 0.5 * wide(rate_ref, b)
        for k in range(KMAX):
            high, low = (part.astype(F32) for part in halves(state))
            stack = jnp.concatenate([high, *gap, low, *gap, high, *gap], axis=0).astype(BF16)
            rate = lax.dot_general(matrix, stack, NN, preferred_element_type=F32)
            state = jnp.where(k < count, state + half * jnp.tanh(rate), state)
        state = jnp.where(row == species, 1.0, state)
        for n in range(group):
            out_ref[b + n] = state[:, n * cells : (n + 1) * cells]


def project_kernel(bins, sp, cells, nshape, groups, accumulate, *refs):
    xs, refs = refs[: len(groups)], refs[len(groups) :]
    key_ref, wc_ref, *refs = refs
    acc_ref = refs.pop(0) if accumulate else None
    out_ref, lhs = refs
    ct = out_ref.shape[1]

    @pl.when(pl.program_id(0) == 0)
    def _():
        for n, x_ref in enumerate(xs):
            high, low = halves(x_ref[...])
            lhs[:, 2 * n * cells : (2 * n + 1) * cells] = high
            lhs[:, (2 * n + 1) * cells : (2 * n + 2) * cells] = low

    cell, _ = decode(key_ref[7:8, :], nshape)
    ids = lax.broadcasted_iota(jnp.int32, (cells, ct), 0)
    hots = []
    for g in groups:
        hot = rows_equal(ids + g * cells, cell)
        hots += [hot, hot]
    y = lax.dot_general(lhs[...], jnp.concatenate(hots, axis=0), NN, preferred_element_type=F32)
    total = acc_ref[...] if accumulate else jnp.zeros((sp, ct), F32)
    for b in range(bins):
        total = total + wc_ref[b + 1 : b + 2, :] * y[b * sp : (b + 1) * sp]
    out_ref[...] = total


def project_call(xs, groups, t, wc, acc, place, count, bins, cells, nshape, ct=256):
    sp, skip = t.shape[0], place // ct
    rows = bins * sp
    whole = lambda shape: pl.BlockSpec(shape, lambda i: (0,) * len(shape))
    col = lambda r: pl.BlockSpec((r, ct), lambda i: (0, i))
    args = list(xs) + [t, wc]
    specs = [whole(x.shape) for x in xs]
    specs.append(pl.BlockSpec((8, ct), lambda i: (sp // 8 - 1, i + skip)))
    specs.append(pl.BlockSpec((wc.shape[0], ct), lambda i: (0, i + skip)))
    if acc is not None:
        args.append(acc)
        specs.append(col(sp))
    return pl.pallas_call(
        functools.partial(project_kernel, bins, sp, cells, nshape, groups, acc is not None),
        grid=(count // ct,),
        out_shape=jax.ShapeDtypeStruct((sp, count), F32),
        in_specs=specs,
        out_specs=col(sp),
        scratch_shapes=[pltpu.VMEM((rows, 2 * len(groups) * cells), BF16)],
        compiler_params=pltpu.CompilerParams(vmem_limit_bytes=40 << 20),
        cost_estimate=pl.CostEstimate(flops=rows * cells * len(groups) * count // 4, bytes_accessed=8 * sp * count, transcendentals=0),
        name="project",
    )(*args)


def on_device(
    les_state, cmc_state, cmc_map, pdf_index, pdf_table, diffusion, chem_matrix, dissipation, reaction_rate, substeps
):
    species = les_state.shape[0]
    sp = -(-(species + 2) // 8) * 8
    own_bins, cells = cmc_state.shape[1:]
    bins = own_bins + 2
    nshape = pdf_table.shape[0]
    count = cmc_map.size
    ncross = lax.axis_size("cross")

    below = shift(les_state[:, -1:], "slab", 1)
    above = shift(les_state[:, :1], "slab", -1)
    behind = shift(les_state[:, :, -1:], "cross", 1)
    ahead = shift(les_state[:, :, :1], "cross", -1)
    xs = jnp.concatenate([below, les_state, above], axis=1)
    ys = jnp.concatenate([behind, les_state, ahead], axis=2)
    zs = jnp.pad(les_state, ((0, 0), (0, 0), (0, 0), (1, 1)))
    around = xs[:, 2:] + xs[:, :-2] + ys[:, :, 2:] + ys[:, :, :-2] + zs[..., 2:] + zs[..., :-2]
    transported = les_state + diffusion[:, None, None, None] * (around - 6.0 * les_state)
    flat = transported.reshape(species, count)
    offset = cmc_map.reshape(1, count) - (lax.axis_index("slab") - 1) * cells
    key = (offset * nshape + pdf_index.reshape(1, count)).astype(F32)
    rows = [flat] + [jnp.ones((1, count), F32)] + [jnp.zeros((sp - species - 2, count), F32)] * (sp > species + 2) + [key]
    t_own = jnp.concatenate(rows, axis=0)

    wb = -(-bins // 8) * 8
    table = jnp.pad(pdf_table.T, ((1, wb - own_bins - 1), (0, 0)))
    table = lax.dynamic_slice_in_dim(table, lax.axis_index("cross") * own_bins, wb, axis=0)
    used = lax.broadcasted_iota(jnp.int32, (wb, 1), 0) < bins
    table = jnp.where(used, table, 0.0)

    cmc_state, t_own = lax.optimization_barrier((cmc_state, t_own))
    left_cells = jnp.concatenate([shift(cmc_state[:, :, -1:], "slab", 1), cmc_state[:, :, :-1]], axis=2)
    right_cells = jnp.concatenate([cmc_state[:, :, 1:], shift(cmc_state[:, :, :1], "slab", -1)], axis=2)
    moved = cmc_state - 0.4 * (cmc_state - left_cells) + 0.1 * (right_cells - 2.0 * cmc_state + left_cells)
    moved = jnp.concatenate(
        [shift(moved[:, -1:], "cross", 1), moved, shift(moved[:, :1], "cross", -1)], axis=1
    )
    moved = jnp.pad(moved.transpose(1, 0, 2), ((0, 0), (0, sp - species), (0, 0)))

    blocks = [t_own]
    bits = [1 << k for k in range(ncross.bit_length() - 1)][::-1]
    for bit in bits:
        got = swap(jnp.concatenate(blocks, axis=1) if len(blocks) > 1 else blocks[0], "cross", bit)
        if len(blocks) == 1:
            got, moved = lax.optimization_barrier((got, moved))
        blocks.append(got)

    acc, wcs = None, []
    for block in blocks:
        acc, wc = bin_call(block, table, None, acc, bins, cells, nshape)
        wcs.append(wc)
    up = shift(acc[:, cells:], "slab", 1)
    down = shift(acc[:, :cells], "slab", -1)
    acc, *wcs = lax.optimization_barrier((acc, *wcs))
    mine = None
    for block, wc in zip(blocks, wcs):
        mine = bin_call(block, table, wc, mine, bins, cells, nshape)

    cube = lambda a: a.reshape(bins, sp, cells)
    extra = sp - species
    fresh = pl.pallas_call(
        functools.partial(chem_kernel, species, sp),
        out_shape=jax.ShapeDtypeStruct((own_bins, sp, cells), F32),
        compiler_params=pltpu.CompilerParams(vmem_limit_bytes=40 << 20),
        name="chem",
    )(
        cube(mine), cube(up), cube(down), moved, dissipation, reaction_rate, substeps[None, :],
        jnp.tile(jnp.pad(chem_matrix, ((0, extra), (0, -(-sp // 16) * 16 - species))), (1, 3)),
    )
    cmc_out = fresh[:, :species].transpose(1, 0, 2)
    fresh = fresh.reshape(own_bins * sp, cells)
    from_below = shift(fresh, "slab", 1)
    from_above = shift(fresh, "slab", -1)

    args = (count, own_bins, cells, nshape)
    where = [(blocks[0], wcs[0], 0)]
    for bit, block, wc in zip(bits, blocks[1:], wcs[1:]):
        held = {r: n for n, r in enumerate(order)} if bit != bits[0] else {0: 0}
        order = list(held) + [r ^ bit for r in held]
        where += [(block, wc, n * count) for n in range(len(held))]
    order = order if bits else [0]
    places = dict(zip(order, where))
    own_part = {r: project_call([fresh], (1,), *places[r][:2], None, places[r][2], *args) for r in order}
    from_below, from_above, own_part = lax.optimization_barrier((from_below, from_above, own_part))

    def reduced(who, bits, sides):
        if not bits:
            block, wc, place = places[who]
            return project_call(sides, (0, 2), block, wc, own_part[who], place, *args)
        far = reduced(who ^ bits[0], bits[1:], sides)
        if len(bits) > 1:
            far, sides = lax.optimization_barrier((far, sides))
        got = swap(far, "cross", bits[0])
        return reduced(who, bits[1:], sides) + got

    total = reduced(0, bits, [from_below, from_above])
    conditional = (total[:species] / total[species : species + 1]).reshape(transported.shape)
    les_out = transported + 0.5 * (conditional - transported)
    return (les_out, cmc_out)


def solution(mesh):
    return jax.shard_map(
        on_device,
        mesh=mesh,
        in_specs=(
            P(None, "slab", "cross", None),
            P(None, "cross", "slab"),
            P("slab", "cross", None),
            P("slab", "cross", None),
            P(),
            P(),
            P(),
            P("cross", "slab"),
            P("cross", "slab"),
            P("slab"),
        ),
        out_specs=(P(None, "slab", "cross", None), P(None, "cross", "slab")),
        check_vma=False,
    )
```
